32 devices in a mesh: rep: 2 (over y), dp: 4 (over x, core), tensor: 4 (over z).
Axes of the slice: x: 2, y: 2, z: 4, core: 2. Of those that a mesh axis runs over, the one named last changes fastest.
Arguments:
- activations: bfloat16 [12288, 8192], P(('rep', 'dp'), 'tensor'), parts along dimension 0, may hold values from -6 to 6
- output_gradient: bfloat16 [12288, 2048], P(('rep', 'dp'), 'tensor'), parts along dimension 0, may hold values from -6 to 6
- row_tenant: int32 [12288, 1], P(('rep', 'dp')), parts along dimension 0, may hold values from 0 to 15; in each aligned block of 1536 rows (0 to 1535, 1536 to 3071, ...) at most 192 rows name the same one
- group_row_count: int32 [8], P(('rep', 'dp')), parts along dimension 0, may hold values from 384 to 1536
- tenant_storage_entry: int32 [16], replicated, may hold values from 0 to 15, each once
- key_value_weight: bfloat16 [8192, 2048], P('tensor'), may hold values from -0.125 to 0.125
- adapter_down_maps: bfloat16 [16, 8192, 64], P('dp', 'tensor'), may hold values from -0.23925781 to 0.23925781
- adapter_up_maps: bfloat16 [16, 64, 2048], P('dp', None, 'tensor'), may hold values from -0.125 to 0.125
- down_row_factor: float32 [16, 8192], P('dp', 'tensor'), may hold values from 2 to 60
- down_column_factor: float32 [16, 64], P('dp'), may hold values from 2 to 60
- up_row_factor: float32 [16, 64], P('dp'), may hold values from 0.02 to 0.6
- up_column_factor: float32 [16, 2048], P('dp', 'tensor'), may hold values from 20 to 600
Outputs:
- input_grad: bfloat16 [12288, 8192], P(('rep', 'dp'), 'tensor'), parts along dimension 0
- down_rows: float32 [32, 8192], P(('rep', 'dp'), 'tensor'), parts along dimension 0
- down_cols: float32 [32, 64], P(('rep', 'dp')), parts along dimension 0
- up_rows: float32 [32, 64], P(('rep', 'dp')), parts along dimension 0
- up_cols: float32 [32, 2048], P(('rep', 'dp'), 'tensor'), parts along dimension 0
- down_update: float32 [32, 8192, 64], P(('rep', 'dp'), 'tensor'), parts along dimension 0
- up_update: float32 [32, 64, 2048], P(('rep', 'dp'), None, 'tensor'), parts along dimension 0
The draws below stay inside these ranges and needn't reach their ends.
There are 2 independent parts, one for each index of `rep`. The reference program is written for one: setup_inputs(seed, part) draws one part's arguments, and reference() takes and returns one part's arrays. A program takes and returns all parts, laid end to end along the dimension named above; an argument that names none is the same for every part. Nothing has to cross between parts.
Inputs may be any that keep to these rules, and one draw needn't show every extreme that they name: `row_tenant`: within the rows of one group (aligned blocks of 1536 rows, padding rows included) no tenant is named by more than 192 rows, a bound that some block reaches. Row 1536 g + i is live for i < group_row_count[g]; the other rows of the group are padding. A permutation: tenant t's adapters and factors are stored at entry tenant_storage_entry[t] of the adapter and factor arrays.
All inputs are finite; a program needn't handle non-finite values.
Results may differ from the reference program's by a relative error of at most 0.0029.
Values may be sent and summed in bfloat16 or wider, within the bound.
A program may use at most 128 MiB of HBM per device.

```python
import math
import jax
import jax.numpy as jnp
import numpy as np
from jax import lax

MODEL_WIDTH = 8192
ADAPTER_RANK = 64
TOK = 1536
KEY_VALUE_WIDTH = 2048
TOKENS = 6144
TENANT_TOTAL = 16
TENANT_ROW_LIMIT = 192
N_DP = 4


def plant(drawn, own_key, low, top_value):
    longest = drawn.shape.index(max(drawn.shape))
    spots = []
    for shift in (0, 1):
        where = [jax.random.randint(jax.random.fold_in(own_key, axis), (), 0, length) for axis, length in enumerate(drawn.shape)]
        where[longest] = (where[longest] + shift) % drawn.shape[longest]
        spots.append(tuple(where))
    return drawn.at[spots[0]].set(low).at[spots[1]].set(top_value)


def block_levels(stream_key, extent, split, smallest, high):
    def one(dim, parts):
        draws = jax.random.uniform(jax.random.fold_in(jax.random.fold_in(stream_key, 6), dim), (parts,), jnp.float32, smallest / len(split), high / len(split))
        return jnp.repeat(jnp.exp(draws), extent[dim] // parts).reshape((-1,) + (1,) * (len(extent) - dim - 1))

    loudness = one(*split[0])
    for cut in split[1:]:
        loudness = loudness * one(*cut)
    return loudness


def shared_out(own_key, own, number, rows, count, top, most, lean):
    ranking = jax.random.permutation(own_key, count)
    heavy_load, ordinary = load_shares(count, rows * top, most, lean, True), load_shares(count, rows * top, most, lean, False)
    places = jnp.arange(count)

    def named(tallies, turn):
        used = int((tallies > 0).sum())
        fixed = max(1, used // 4)
        moved = fixed + (places - fixed + turn * (used - fixed)) % max(1, count - fixed)
        return jnp.zeros((count,), jnp.int32).at[ranking[jnp.where(places < fixed, places, moved)]].set(jnp.asarray(tallies, jnp.int32))

    tallies = jnp.where(number % 4 == 0, named(heavy_load, number // 4), named(ordinary, number - number // 4 - 1))
    mixed = jax.random.permutation(jax.random.fold_in(own, 3), count)
    source_of, taker = mixed[0:count // 2 * 2:2], mixed[1:count // 2 * 2:2]
    margin = jnp.minimum(tallies[source_of] - 1, most - tallies[taker]) // 2
    margin = jnp.where((source_of == ranking[0]) | (taker == ranking[0]) | (tallies[taker] == 0), 0, jnp.maximum(margin, 0))
    moved = jax.random.randint(jax.random.fold_in(own, 4), (count // 2,), 0, 1 << 20) % (margin + 1)
    tallies = tallies.at[source_of].add(-moved).at[taker].add(moved)
    members = jnp.searchsorted(jnp.cumsum(tallies), jnp.arange(rows * top), side="right").astype(jnp.int32)
    table = members.reshape(top, rows).T
    table = table[jax.random.permutation(jax.random.fold_in(own, 1), rows)]
    turn = jax.random.randint(jax.random.fold_in(own, 2), (rows, 1), 0, top)
    return jnp.take_along_axis(table, (jnp.arange(top)[None, :] + turn) % top, axis=1)


def load_shares(number_of, total, limit, skew, full):
    portions = [(1 << 20) // math.isqrt(rank ** skew) + 1 for rank in range(1, number_of + 1)]
    largest = limit if full else min(limit, max(-(-total // number_of), total * portions[0] // sum(portions)))
    least = 1 if total - largest >= number_of - 1 else 0
    given, spare = [largest] + [least] * (number_of - 1), total - largest - least * (number_of - 1)
    while spare > 0:
        free = [i for i in range(1, number_of) if given[i] < largest] or [i for i in range(1, number_of) if given[i] < limit]
        whole, remaining = sum([portions[i] for i in free]), spare
        for i in free:
            more = min(limit - given[i], max(1, remaining * portions[i] // whole), spare)
            given[i] = given[i] + more
            spare = spare - more
    return np.array(given)


def bell_draw(rng, dims, spread, bound, shards=(), kind=jnp.bfloat16):
    drawn = jax.random.normal(rng, dims, jnp.float32) * spread
    if len(shards) > 0:
        drawn = block_levels(rng, dims, shards, -0.22, 0.18) * drawn
    return jnp.clip(drawn, min=-bound, max=bound).astype(kind)


def setup_inputs(seed: int = 0, part: int = 0) -> dict:
    splits = jax.random.split(jax.random.key(seed), 13)
    part_keys = jax.random.split(jax.random.fold_in(splits[12], part), 13)
    activations = bell_draw(part_keys[0], (TOKENS, MODEL_WIDTH), 1.0, 6.0, ((0, 4), (1, 4)))
    output_gradient = bell_draw(part_keys[1], (TOKENS, KEY_VALUE_WIDTH), 1.0, 6.0, ((0, 4), (1, 4)))
    row_tenant_keys = jax.random.split(jax.random.fold_in(part_keys[2], 1), TOKENS // TOK)
    row_tenant_turns = jax.random.permutation(jax.random.fold_in(part_keys[2], 3), TOKENS // TOK)
    row_tenant = jax.vmap(lambda own, number: shared_out(jax.random.fold_in(part_keys[2], 2), own, number, TOK, TENANT_TOTAL, 1, TENANT_ROW_LIMIT, 2))(row_tenant_keys, row_tenant_turns).reshape((TOKENS, 1))
    group_row_count = plant(jax.random.randint(part_keys[3], (N_DP,), TOK // 4, TOK + 1), jax.random.fold_in(part_keys[3], 1), TOK // 4, TOK).astype(jnp.int32)
    tenant_storage_entry = jax.random.permutation(splits[4], TENANT_TOTAL).astype(jnp.int32)
    key_value_weight = bell_draw(splits[5], (MODEL_WIDTH, KEY_VALUE_WIDTH), KEY_VALUE_WIDTH ** -0.5, 0.125, ((0, 4),))
    adapter_down_maps = bell_draw(splits[6], (TENANT_TOTAL, MODEL_WIDTH, ADAPTER_RANK), 0.04, 0.23925781, ((0, 4), (1, 4)))
    adapter_up_maps = bell_draw(splits[7], (TENANT_TOTAL, ADAPTER_RANK, KEY_VALUE_WIDTH), KEY_VALUE_WIDTH ** -0.5, 0.125, ((0, 4), (2, 4)))
    down_row_factor = jnp.clip(jnp.exp(math.log(60.0) - 3.4011974 * jax.random.uniform(splits[8], (TENANT_TOTAL, MODEL_WIDTH), jnp.float32) ** block_levels(splits[8], (TENANT_TOTAL, MODEL_WIDTH), ((0, 4), (1, 4)), -0.2, 0.2)), 2.0, 60.0)
    down_column_factor = jnp.clip(jnp.exp(math.log(60.0) - 3.4011974 * jax.random.uniform(splits[9], (TENANT_TOTAL, ADAPTER_RANK), jnp.float32) ** block_levels(splits[9], (TENANT_TOTAL, ADAPTER_RANK), ((0, 4),), -0.2, 0.2)), 2.0, 60.0)
    up_row_factor = jnp.clip(jnp.exp(math.log(0.6) - 3.4011974 * jax.random.uniform(splits[10], (TENANT_TOTAL, ADAPTER_RANK), jnp.float32) ** block_levels(splits[10], (TENANT_TOTAL, ADAPTER_RANK), ((0, 4),), -0.2, 0.2)), 0.02, 0.6)
    up_column_factor = jnp.clip(jnp.exp(math.log(600.0) - 3.4011974 * jax.random.uniform(splits[11], (TENANT_TOTAL, KEY_VALUE_WIDTH), jnp.float32) ** block_levels(splits[11], (TENANT_TOTAL, KEY_VALUE_WIDTH), ((0, 4), (1, 4)), -0.2, 0.2)), 20.0, 600.0)
    return dict(activations=activations, output_gradient=output_gradient, row_tenant=row_tenant, group_row_count=group_row_count, tenant_storage_entry=tenant_storage_entry, key_value_weight=key_value_weight, adapter_down_maps=adapter_down_maps, adapter_up_maps=adapter_up_maps, down_row_factor=down_row_factor, down_column_factor=down_column_factor, up_row_factor=up_row_factor, up_column_factor=up_column_factor)


adapter_scale = 0.25
decay_rate = 0.9
tiny_floor = 1e-30

def slot_layout(tenant_col, tenant_storage_entry, row_limit):
    tenants = tenant_col[:, 0]
    count_rows = tenants.shape[0]
    entries = tenant_storage_entry.shape[0]
    onehot = (tenants[:, None] == jnp.arange(entries, dtype=jnp.int32)[None, :]).astype(jnp.int32)
    position = jnp.cumsum(onehot, axis=0) - onehot
    within = lax.optimization_barrier(jnp.sum(position * onehot, axis=1)).astype(jnp.int32)
    entry_of = lax.optimization_barrier(jnp.sum(onehot * tenant_storage_entry[None, :], axis=1)).astype(jnp.int32)
    target = (entry_of * row_limit + within).astype(jnp.int32)
    lookup = jnp.full((entries * row_limit,), count_rows, jnp.int32).at[target].set(jnp.arange(count_rows, dtype=jnp.int32))
    return (target, lookup)

def reference(activations, output_gradient, row_tenant, group_row_count, tenant_storage_entry, key_value_weight, adapter_down_maps, adapter_up_maps, down_row_factor, down_column_factor, up_row_factor, up_column_factor):
    live_mask = (jnp.arange(TOK, dtype=jnp.int32)[None, :] < group_row_count[:, None]).reshape(TOKENS, 1)
    masked = jnp.where(live_mask, output_gradient, jnp.zeros_like(output_gradient))
    frozen = jnp.dot(masked, key_value_weight.T, preferred_element_type=jnp.float32)
    target, lookup = jax.vmap(lambda column: slot_layout(column, tenant_storage_entry, TENANT_ROW_LIMIT))(row_tenant.reshape(N_DP, TOK, 1))
    padded_x = jnp.concatenate([activations.reshape(N_DP, TOK, MODEL_WIDTH), jnp.zeros((N_DP, 1, MODEL_WIDTH), activations.dtype)], axis=1)
    padded_g = jnp.concatenate([masked.reshape(N_DP, TOK, KEY_VALUE_WIDTH), jnp.zeros((N_DP, 1, KEY_VALUE_WIDTH), masked.dtype)], axis=1)
    group_numbers = jnp.arange(N_DP, dtype=jnp.int32)[:, None]

    def per_entry(written_rows, entry_number):
        storage_index = lax.dynamic_slice_in_dim(lookup, entry_number * TENANT_ROW_LIMIT, TENANT_ROW_LIMIT, 1)
        picked_input = padded_x[group_numbers, storage_index].reshape(N_DP * TENANT_ROW_LIMIT, MODEL_WIDTH)
        picked_gradient = padded_g[group_numbers, storage_index].reshape(N_DP * TENANT_ROW_LIMIT, KEY_VALUE_WIDTH)
        down_entry_map = adapter_down_maps[entry_number]
        up_entry_map = adapter_up_maps[entry_number]
        proj_down = jnp.dot(picked_input, down_entry_map, preferred_element_type=jnp.float32)
        proj_up = jnp.dot(picked_gradient, up_entry_map.T, preferred_element_type=jnp.float32)
        rounded_down = proj_down.astype(jnp.bfloat16)
        rounded_up = proj_up.astype(jnp.bfloat16)
        down_gradient = adapter_scale * jnp.dot(picked_input.T, rounded_up, preferred_element_type=jnp.float32)
        up_gradient = adapter_scale * jnp.dot(rounded_down.T, picked_gradient, preferred_element_type=jnp.float32)
        adapter_branch = (adapter_scale * jnp.dot(rounded_up, down_entry_map.T, preferred_element_type=jnp.float32)).astype(jnp.bfloat16)
        written_rows = written_rows.at[group_numbers, storage_index].set(adapter_branch.reshape(N_DP, TENANT_ROW_LIMIT, MODEL_WIDTH))
        return (written_rows, (down_gradient, up_gradient))
    blank_rows = jnp.zeros((N_DP, TOK + 1, MODEL_WIDTH), jnp.bfloat16)
    side_all, grads = lax.scan(per_entry, blank_rows, jnp.arange(TENANT_TOTAL, dtype=jnp.int32))
    down_gradient, up_gradient = grads
    side_rows = side_all[:, :TOK, :].reshape(TOKENS, MODEL_WIDTH)
    input_grad = (frozen + side_rows.astype(jnp.float32)).astype(jnp.bfloat16)
    square_down = down_gradient * down_gradient + tiny_floor
    square_up = up_gradient * up_gradient + tiny_floor
    down_rows = decay_rate * down_row_factor + (1.0 - decay_rate) * lax.optimization_barrier(jnp.mean(square_down, axis=2))
    down_cols = decay_rate * down_column_factor + (1.0 - decay_rate) * lax.optimization_barrier(jnp.mean(square_down, axis=1))
    up_rows = decay_rate * up_row_factor + (1.0 - decay_rate) * lax.optimization_barrier(jnp.mean(square_up, axis=2))
    up_cols = decay_rate * up_column_factor + (1.0 - decay_rate) * lax.optimization_barrier(jnp.mean(square_up, axis=1))
    second_down = down_rows[:, :, None] * down_cols[:, None, :] / lax.optimization_barrier(jnp.mean(down_rows, axis=1))[:, None, None]
    second_up = up_rows[:, :, None] * up_cols[:, None, :] / lax.optimization_barrier(jnp.mean(up_rows, axis=1))[:, None, None]
    down_update = down_gradient * lax.rsqrt(second_down)
    up_update = up_gradient * lax.rsqrt(second_up)
    return (input_grad, down_rows, down_cols, up_rows, up_cols, down_update, up_update)
```

```python
import jax
import jax.numpy as jnp
from jax import lax
from jax.sharding import PartitionSpec as P

adapter_scale = 0.25
decay_rate = 0.9
tiny_floor = 1e-30
f32 = jnp.float32
bf16 = jnp.bfloat16
CORES = 2


def dot(a, b, ca, cb):
    return lax.dot_general(a, b, (((ca,), (cb,)), ((), ())), preferred_element_type=f32)


def chip_shift(value, groups, step):
    chips = groups // CORES
    pairs = [(d, (d // CORES + step) % chips * CORES + d % CORES) for d in range(groups)]
    return lax.ppermute(value, "dp", pairs)


def core_swap(value, groups):
    return lax.ppermute(value, "dp", [(d, d ^ 1) for d in range(groups)])


def ring_shift(value, size, step):
    return lax.ppermute(value, "tensor", [(t, (t + step) % size) for t in range(size)])


def total_small(value, size):
    if size > 8:
        return lax.psum(value, "tensor")
    me = lax.axis_index("tensor")
    parts = jnp.zeros((size,) + value.shape, value.dtype)
    parts = lax.dynamic_update_index_in_dim(parts, value, me, 0)
    for step in range(1, size):
        got = ring_shift(value, size, step)
        parts = lax.dynamic_update_index_in_dim(parts, got, (me - step) % size, 0)
    return jnp.sum(parts, axis=0)


def total_rows(value, size):
    if size > 8:
        return lax.psum(value, "tensor").astype(bf16)
    me = lax.axis_index("tensor")
    rows = value.shape[0] // size

    def piece(index):
        return lax.dynamic_slice_in_dim(value, index % size * rows, rows, 0)

    total = piece(me)
    for step in range(1, size):
        total = total + ring_shift(piece(me + step), size, step)
    mine = total.astype(bf16)
    out = jnp.zeros(value.shape, bf16)
    out = lax.dynamic_update_slice_in_dim(out, mine, me * rows, 0)
    for step in range(1, size):
        got = ring_shift(mine, size, step)
        out = lax.dynamic_update_slice_in_dim(out, got, (me - step) % size * rows, 0)
    return out


def shards(
    activations,
    output_gradient,
    row_tenant,
    group_row_count,
    tenant_storage_entry,
    key_value_weight,
    adapter_down_maps,
    adapter_up_maps,
    down_row_factor,
    down_column_factor,
    up_row_factor,
    up_column_factor,
):
    groups = lax.axis_size("dp")
    size = lax.axis_size("tensor")
    chips = groups // CORES
    owned, depth, rank = adapter_down_maps.shape
    width = adapter_up_maps.shape[2]
    entries = owned * groups
    count_rows = activations.shape[0]
    full_width = depth * size
    pair_width = key_value_weight.shape[1]
    here = lax.axis_index("dp")
    chip, core = here // CORES, here % CORES
    gathered = lax.all_gather(output_gradient, "tensor", axis=1, tiled=True)
    own_maps = jnp.concatenate(
        [adapter_down_maps.transpose(0, 2, 1), adapter_up_maps], axis=2
    ).reshape(owned * rank, depth + width)
    blocks = []
    for s in range(chips):
        column = own_maps if s == 0 else chip_shift(own_maps, groups, s)
        blocks.append(jnp.concatenate([column, core_swap(column, groups)], axis=0))
    live = jnp.arange(count_rows, dtype=jnp.int32)[:, None] < group_row_count[0]
    masked = jnp.where(live, output_gradient, jnp.zeros_like(output_gradient))
    tse = tenant_storage_entry
    owner = tse // owned
    place = (
        (chip - owner // CORES) % chips * CORES + (owner % CORES != core).astype(jnp.int32)
    ) * owned + tse % owned
    tenants = row_tenant[:, 0]
    place_of = jnp.sum(
        jnp.where(
            tenants[:, None] == jnp.arange(entries, dtype=jnp.int32)[None, :], place[None, :], 0
        ),
        axis=1,
    )
    span = CORES * owned * rank
    pair = 2 * rank
    lanes = jnp.arange(span, dtype=jnp.int32)[None, :] // rank

    def wide(s):
        return place_of[:, None] == lanes + s * CORES * owned

    def pick(s, product):
        kept = jnp.where(wide(s), product, 0.0)
        both = kept[:, :pair]
        for i in range(1, span // pair):
            both = both + kept[:, i * pair : (i + 1) * pair]
        return both

    picked_down = picked_up = 0.0
    for s in range(chips):
        picked_down += pick(s, dot(activations, blocks[s][:, :depth], 1, 1))
        picked_up += pick(s, dot(masked, blocks[s][:, depth:], 1, 1))
    partial = jnp.concatenate(
        [
            picked_down[:, :rank] + picked_down[:, rank:],
            picked_up[:, :rank] + picked_up[:, rank:],
        ],
        axis=1,
    )
    rounded = total_rows(partial, size)
    zero = jnp.zeros((), bf16)
    repeat_down = jnp.tile(rounded[:, :rank], (1, span // rank))
    repeat_up = jnp.tile(rounded[:, rank:], (1, span // rank))
    half = owned * rank
    grads = 0.0
    spreads = [None] * chips
    for s in list(range(1, chips)) + [0]:
        spreads[s] = jnp.where(wide(s), repeat_up, zero)
        spread_down = jnp.where(wide(s), repeat_down, zero)
        terms = adapter_scale * jnp.concatenate(
            [dot(spreads[s], activations, 0, 0), dot(spread_down, masked, 0, 0)], axis=1
        )
        summed = terms[:half] + core_swap(terms[half:], groups)
        if s:
            summed = chip_shift(summed.astype(bf16), groups, -s).astype(f32)
        grads = grads + summed
    grads = grads.reshape(owned, rank, depth + width)
    down_gradient, up_gradient = grads[:, :, :depth], grads[:, :, depth:]
    frozen = jnp.where(live, dot(gathered, key_value_weight, 1, 1), 0.0)
    side = (
        adapter_scale
        * dot(
            jnp.concatenate(spreads, axis=1),
            jnp.concatenate([b[:, :depth] for b in blocks], axis=0),
            1,
            0,
        )
    ).astype(bf16)
    input_grad = (frozen + side.astype(f32)).astype(bf16)
    square_down = down_gradient * down_gradient + tiny_floor
    square_up = up_gradient * up_gradient + tiny_floor
    down_rows = decay_rate * down_row_factor + (1.0 - decay_rate) * jnp.mean(square_down, axis=1)
    up_cols = decay_rate * up_column_factor + (1.0 - decay_rate) * jnp.mean(square_up, axis=1)
    stats = jnp.concatenate(
        [
            jnp.sum(square_down, axis=2),
            jnp.sum(square_up, axis=2),
            jnp.broadcast_to(jnp.sum(down_rows, axis=1)[:, None], (owned, pair)),
        ],
        axis=1,
    )
    stats = total_small(stats, size)
    column_total, row_total = stats[:, :rank], stats[:, rank:pair]
    rows_sum = stats[:, pair]
    down_cols = decay_rate * down_column_factor + (1.0 - decay_rate) * (column_total / full_width)
    up_rows = decay_rate * up_row_factor + (1.0 - decay_rate) * (row_total / pair_width)
    second_down = (
        down_rows[:, None, :] * down_cols[:, :, None] / (rows_sum / full_width)[:, None, None]
    )
    second_up = up_rows[:, :, None] * up_cols[:, None, :] / jnp.mean(up_rows, axis=1)[:, None, None]
    down_update = (down_gradient * lax.rsqrt(second_down)).transpose(0, 2, 1)
    up_update = up_gradient * lax.rsqrt(second_up)
    return (input_grad, down_rows, down_cols, up_rows, up_cols, down_update, up_update)


def solution(mesh):
    in_specs = (
        P(("rep", "dp"), "tensor"),
        P(("rep", "dp"), "tensor"),
        P(("rep", "dp"), None),
        P(("rep", "dp")),
        P(),
        P("tensor", None),
        P("dp", "tensor", None),
        P("dp", None, "tensor"),
        P("dp", "tensor"),
        P("dp", None),
        P("dp", None),
        P("dp", "tensor"),
    )
    out_specs = (
        P(("rep", "dp"), "tensor"),
        P(("rep", "dp"), "tensor"),
        P(("rep", "dp"), None),
        P(("rep", "dp"), None),
        P(("rep", "dp"), "tensor"),
        P(("rep", "dp"), "tensor", None),
        P(("rep", "dp"), None, "tensor"),
    )
    return jax.shard_map(shards, mesh=mesh, in_specs=in_specs, out_specs=out_specs, check_vma=False)
```

```python
import jax
import jax.numpy as jnp
from jax import lax
from jax.sharding import PartitionSpec as P

adapter_scale = 0.25
decay_rate = 0.9
tiny_floor = 1e-30
f32 = jnp.float32
bf16 = jnp.bfloat16
CORES = 2


def dot(a, b, ca, cb):
    return lax.dot_general(a, b, (((ca,), (cb,)), ((), ())), preferred_element_type=f32)


def chip_shift(value, groups, step):
    chips = groups // CORES
    pairs = [(d, (d // CORES + step) % chips * CORES + d % CORES) for d in range(groups)]
    return lax.ppermute(value, "dp", pairs)


def core_swap(value, groups):
    return lax.ppermute(value, "dp", [(d, d ^ 1) for d in range(groups)])


def ring_shift(value, size, step):
    return lax.ppermute(value, "tensor", [(t, (t + step) % size) for t in range(size)])


def total_small(value, size):
    if size > 8:
        return lax.psum(value, "tensor")
    me = lax.axis_index("tensor")
    parts = jnp.zeros((size,) + value.shape, value.dtype)
    parts = lax.dynamic_update_index_in_dim(parts, value, me, 0)
    for step in range(1, size):
        got = ring_shift(value, size, step)
        parts = lax.dynamic_update_index_in_dim(parts, got, (me - step) % size, 0)
    return jnp.sum(parts, axis=0)


def total_rows(value, size):
    if size > 8:
        return lax.psum(value, "tensor").astype(bf16)
    me = lax.axis_index("tensor")
    rows = value.shape[0] // size

    def piece(index):
        return lax.dynamic_slice_in_dim(value, index % size * rows, rows, 0)

    total = piece(me)
    for step in range(1, size):
        total = total + ring_shift(piece(me + step), size, step)
    mine = total.astype(bf16)
    out = jnp.zeros(value.shape, bf16)
    out = lax.dynamic_update_slice_in_dim(out, mine, me * rows, 0)
    for step in range(1, size):
        got = ring_shift(mine, size, step)
        out = lax.dynamic_update_slice_in_dim(out, got, (me - step) % size * rows, 0)
    return out


def shards(
    activations,
    output_gradient,
    row_tenant,
    group_row_count,
    tenant_storage_entry,
    key_value_weight,
    adapter_down_maps,
    adapter_up_maps,
    down_row_factor,
    down_column_factor,
    up_row_factor,
    up_column_factor,
):
    groups = lax.axis_size("dp")
    size = lax.axis_size("tensor")
    chips = groups // CORES
    owned, depth, rank = adapter_down_maps.shape
    width = adapter_up_maps.shape[2]
    entries = owned * groups
    count_rows = activations.shape[0]
    full_width = depth * size
    pair_width = key_value_weight.shape[1]
    here = lax.axis_index("dp")
    chip, core = here // CORES, here % CORES
    gathered = lax.all_gather(output_gradient, "tensor", axis=1, tiled=True)
    own_maps = jnp.concatenate(
        [adapter_down_maps.transpose(0, 2, 1), adapter_up_maps], axis=2
    ).reshape(owned * rank, depth + width)
    blocks = []
    for s in range(chips):
        column = own_maps if s == 0 else chip_shift(own_maps, groups, s)
        blocks.append(jnp.concatenate([column, core_swap(column, groups)], axis=0))
    live = jnp.arange(count_rows, dtype=jnp.int32)[:, None] < group_row_count[0]
    masked = jnp.where(live, output_gradient, jnp.zeros_like(output_gradient))
    tse = tenant_storage_entry
    owner = tse // owned
    place = (
        (chip - owner // CORES) % chips * CORES + (owner % CORES != core).astype(jnp.int32)
    ) * owned + tse % owned
    tenants = row_tenant[:, 0]
    place_of = jnp.sum(
        jnp.where(
            tenants[:, None] == jnp.arange(entries, dtype=jnp.int32)[None, :], place[None, :], 0
        ),
        axis=1,
    )
    span = CORES * owned * rank
    pair = 2 * rank
    lanes = jnp.arange(span, dtype=jnp.int32)[None, :] // rank

    def wide(s):
        return place_of[:, None] == lanes + s * CORES * owned

    def pick(s, product):
        kept = jnp.where(wide(s), product, 0.0)
        both = kept[:, :pair]
        for i in range(1, span // pair):
            both = both + kept[:, i * pair : (i + 1) * pair]
        return both

    picked_down = picked_up = 0.0
    for s in range(chips):
        picked_down += pick(s, dot(activations, blocks[s][:, :depth], 1, 1))
        picked_up += pick(s, dot(masked, blocks[s][:, depth:], 1, 1))
    partial = jnp.concatenate(
        [
            picked_down[:, :rank] + picked_down[:, rank:],
            picked_up[:, :rank] + picked_up[:, rank:],
        ],
        axis=1,
    )
    rounded = total_rows(partial, size)
    zero = jnp.zeros((), bf16)
    repeat_down = jnp.tile(rounded[:, :rank], (1, span // rank))
    repeat_up = jnp.tile(rounded[:, rank:], (1, span // rank))
    half = owned * rank
    spreads = [jnp.where(wide(s), repeat_up, zero) for s in range(chips)]
    pieces = []
    for s in list(range(1, chips)) + [0]:
        spread_down = jnp.where(wide(s), repeat_down, zero)
        terms = [
            adapter_scale
            * jnp.concatenate(
                [
                    dot(spreads[s][:, k : k + half], activations, 0, 0),
                    dot(spread_down[:, k : k + half], masked, 0, 0),
                ],
                axis=1,
            )
            for k in (half, 0)
        ]
        summed = terms[1] + core_swap(terms[0], groups)
        pieces.append(chip_shift(summed.astype(bf16), groups, -s) if s else summed)
    side = lax.optimization_barrier(
        (
            adapter_scale
            * dot(
                jnp.concatenate(spreads, axis=1),
                jnp.concatenate([b[:, :depth] for b in blocks], axis=0),
                1,
                0,
            )
        ).astype(bf16)
    )
    frozen = jnp.where(live, dot(gathered, key_value_weight, 1, 1), 0.0)
    input_grad = (frozen + side.astype(f32)).astype(bf16)
    pieces, input_grad = lax.optimization_barrier((pieces, input_grad))
    grads = sum(p.astype(f32) for p in pieces)
    grads = grads.reshape(owned, rank, depth + width)
    down_gradient, up_gradient = grads[:, :, :depth], grads[:, :, depth:]
    square_down = down_gradient * down_gradient + tiny_floor
    square_up = up_gradient * up_gradient + tiny_floor
    down_rows = decay_rate * down_row_factor + (1.0 - decay_rate) * jnp.mean(square_down, axis=1)
    up_cols = decay_rate * up_column_factor + (1.0 - decay_rate) * jnp.mean(square_up, axis=1)
    stats = jnp.concatenate(
        [
            jnp.sum(square_down, axis=2),
            jnp.sum(square_up, axis=2),
            jnp.broadcast_to(jnp.sum(down_rows, axis=1)[:, None], (owned, pair)),
        ],
        axis=1,
    )
    stats = total_small(stats, size)
    column_total, row_total = stats[:, :rank], stats[:, rank:pair]
    rows_sum = stats[:, pair]
    down_cols = decay_rate * down_column_factor + (1.0 - decay_rate) * (column_total / full_width)
    up_rows = decay_rate * up_row_factor + (1.0 - decay_rate) * (row_total / pair_width)
    second_down = (
        down_rows[:, None, :] * down_cols[:, :, None] / (rows_sum / full_width)[:, None, None]
    )
    second_up = up_rows[:, :, None] * up_cols[:, None, :] / jnp.mean(up_rows, axis=1)[:, None, None]
    down_update = (down_gradient * lax.rsqrt(second_down)).transpose(0, 2, 1)
    up_update = up_gradient * lax.rsqrt(second_up)
    return (input_grad, down_rows, down_cols, up_rows, up_cols, down_update, up_update)


def solution(mesh):
    in_specs = (
        P(("rep", "dp"), "tensor"),
        P(("rep", "dp"), "tensor"),
        P(("rep", "dp"), None),
        P(("rep", "dp")),
        P(),
        P("tensor", None),
        P("dp", "tensor", None),
        P("dp", None, "tensor"),
        P("dp", "tensor"),
        P("dp", None),
        P("dp", None),
        P("dp", "tensor"),
    )
    out_specs = (
        P(("rep", "dp"), "tensor"),
        P(("rep", "dp"), "tensor"),
        P(("rep", "dp"), None),
        P(("rep", "dp"), None),
        P(("rep", "dp"), "tensor"),
        P(("rep", "dp"), "tensor", None),
        P(("rep", "dp"), None, "tensor"),
    )
    return jax.shard_map(shards, mesh=mesh, in_specs=in_specs, out_specs=out_specs, check_vma=False)
```

```python
import jax
import jax.numpy as jnp
from jax import lax
from jax.sharding import PartitionSpec as P

adapter_scale = 0.25
decay_rate = 0.9
tiny_floor = 1e-30
f32 = jnp.float32
bf16 = jnp.bfloat16
CORES = 2


def dot(a, b, ca, cb):
    return lax.dot_general(a, b, (((ca,), (cb,)), ((), ())), preferred_element_type=f32)


def chip_shift(value, groups, step):
    chips = groups // CORES
    pairs = [(d, (d // CORES + step) % chips * CORES + d % CORES) for d in range(groups)]
    return lax.ppermute(value, "dp", pairs)


def core_swap(value, groups):
    return lax.ppermute(value, "dp", [(d, d ^ 1) for d in range(groups)])


def ring_shift(value, size, step):
    return lax.ppermute(value, "tensor", [(t, (t + step) % size) for t in range(size)])


def total_small(value, size):
    if size > 8:
        return lax.psum(value, "tensor")
    me = lax.axis_index("tensor")
    parts = jnp.zeros((size,) + value.shape, value.dtype)
    parts = lax.dynamic_update_index_in_dim(parts, value, me, 0)
    for step in range(1, size):
        got = ring_shift(value, size, step)
        parts = lax.dynamic_update_index_in_dim(parts, got, (me - step) % size, 0)
    return jnp.sum(parts, axis=0)


def total_rows(value, size):
    if size > 8:
        return lax.psum(value, "tensor").astype(bf16)
    me = lax.axis_index("tensor")
    rows = value.shape[0] // size

    def piece(index):
        return lax.dynamic_slice_in_dim(value, index % size * rows, rows, 0)

    total = piece(me)
    for step in range(1, size):
        total = total + ring_shift(piece(me + step), size, step)
    mine = total.astype(bf16)
    out = jnp.zeros(value.shape, bf16)
    out = lax.dynamic_update_slice_in_dim(out, mine, me * rows, 0)
    for step in range(1, size):
        got = ring_shift(mine, size, step)
        out = lax.dynamic_update_slice_in_dim(out, got, (me - step) % size * rows, 0)
    return out


def shards(
    activations,
    output_gradient,
    row_tenant,
    group_row_count,
    tenant_storage_entry,
    key_value_weight,
    adapter_down_maps,
    adapter_up_maps,
    down_row_factor,
    down_column_factor,
    up_row_factor,
    up_column_factor,
):
    groups = lax.axis_size("dp")
    size = lax.axis_size("tensor")
    chips = groups // CORES
    owned, depth, rank = adapter_down_maps.shape
    width = adapter_up_maps.shape[2]
    entries = owned * groups
    count_rows = activations.shape[0]
    full_width = depth * size
    pair_width = key_value_weight.shape[1]
    here = lax.axis_index("dp")
    chip, core = here // CORES, here % CORES
    gathered = lax.all_gather(output_gradient, "tensor", axis=1, tiled=True)
    own_maps = jnp.concatenate(
        [adapter_down_maps.transpose(0, 2, 1), adapter_up_maps], axis=2
    ).reshape(owned * rank, depth + width)
    columns = [own_maps] + [chip_shift(own_maps, groups, s) for s in range(1, chips)]
    live = jnp.arange(count_rows, dtype=jnp.int32)[:, None] < group_row_count[0]
    masked = jnp.where(live, output_gradient, jnp.zeros_like(output_gradient))
    tse = tenant_storage_entry
    owner = tse // owned
    place = (
        (chip - owner // CORES) % chips * CORES + (owner % CORES != core).astype(jnp.int32)
    ) * owned + tse % owned
    tenants = row_tenant[:, 0]
    place_of = jnp.sum(
        jnp.where(
            tenants[:, None] == jnp.arange(entries, dtype=jnp.int32)[None, :], place[None, :], 0
        ),
        axis=1,
    )
    span = CORES * owned * rank
    pair = 2 * rank
    lanes = jnp.arange(span, dtype=jnp.int32)[None, :] // rank

    def wide(s):
        return place_of[:, None] == lanes + s * CORES * owned

    def pick(s, product):
        kept = jnp.where(wide(s), product, 0.0)
        both = kept[:, :pair]
        for i in range(1, span // pair):
            both = both + kept[:, i * pair : (i + 1) * pair]
        return both

    blocks = []
    picked_down = picked_up = 0.0
    for s in range(chips):
        column = columns[s]
        if s:
            column, picked_down, picked_up = lax.optimization_barrier(
                (column, picked_down, picked_up)
            )
        blocks.append(jnp.concatenate([column, core_swap(column, groups)], axis=0))
        picked_down += pick(s, dot(activations, blocks[s][:, :depth], 1, 1))
        picked_up += pick(s, dot(masked, blocks[s][:, depth:], 1, 1))
    partial = jnp.concatenate(
        [
            picked_down[:, :rank] + picked_down[:, rank:],
            picked_up[:, :rank] + picked_up[:, rank:],
        ],
        axis=1,
    )
    rounded = total_rows(partial, size)
    zero = jnp.zeros((), bf16)
    repeat_down = jnp.tile(rounded[:, :rank], (1, span // rank))
    repeat_up = jnp.tile(rounded[:, rank:], (1, span // rank))
    half = owned * rank
    spreads = [jnp.where(wide(s), repeat_up, zero) for s in range(chips)]
    pieces = []
    for s in list(range(1, chips)) + [0]:
        spread_down = jnp.where(wide(s), repeat_down, zero)
        terms = [
            adapter_scale
            * jnp.concatenate(
                [
                    dot(spreads[s][:, k : k + half], activations, 0, 0),
                    dot(spread_down[:, k : k + half], masked, 0, 0),
                ],
                axis=1,
            )
            for k in (half, 0)
        ]
        summed = terms[1] + core_swap(terms[0], groups)
        if s:
            summed, spreads = lax.optimization_barrier((summed.astype(bf16), spreads))
            summed = chip_shift(summed, groups, -s)
        pieces.append(summed)
    side = lax.optimization_barrier(
        (
            adapter_scale
            * dot(
                jnp.concatenate(spreads, axis=1),
                jnp.concatenate([b[:, :depth] for b in blocks], axis=0),
                1,
                0,
            )
        ).astype(bf16)
    )
    grads = sum(p.astype(f32) for p in pieces)
    grads = grads.reshape(owned, rank, depth + width)
    down_gradient, up_gradient = grads[:, :, :depth], grads[:, :, depth:]
    square_down = down_gradient * down_gradient + tiny_floor
    square_up = up_gradient * up_gradient + tiny_floor
    down_rows = decay_rate * down_row_factor + (1.0 - decay_rate) * jnp.mean(square_down, axis=1)
    up_cols = decay_rate * up_column_factor + (1.0 - decay_rate) * jnp.mean(square_up, axis=1)
    stats = jnp.concatenate(
        [
            jnp.sum(square_down, axis=2),
            jnp.sum(square_up, axis=2),
            jnp.broadcast_to(jnp.sum(down_rows, axis=1)[:, None], (owned, pair)),
        ],
        axis=1,
    )
    stats, gathered = lax.optimization_barrier((stats, gathered))
    frozen = jnp.where(live, dot(gathered, key_value_weight, 1, 1), 0.0)
    input_grad = (frozen + side.astype(f32)).astype(bf16)
    stats, input_grad = lax.optimization_barrier((total_small(stats, size), input_grad))
    column_total, row_total = stats[:, :rank], stats[:, rank:pair]
    rows_sum = stats[:, pair]
    down_cols = decay_rate * down_column_factor + (1.0 - decay_rate) * (column_total / full_width)
    up_rows = decay_rate * up_row_factor + (1.0 - decay_rate) * (row_total / pair_width)
    second_down = (
        down_rows[:, None, :] * down_cols[:, :, None] / (rows_sum / full_width)[:, None, None]
    )
    second_up = up_rows[:, :, None] * up_cols[:, None, :] / jnp.mean(up_rows, axis=1)[:, None, None]
    down_update = (down_gradient * lax.rsqrt(second_down)).transpose(0, 2, 1)
    up_update = up_gradient * lax.rsqrt(second_up)
    return (input_grad, down_rows, down_cols, up_rows, up_cols, down_update, up_update)


def solution(mesh):
    in_specs = (
        P(("rep", "dp"), "tensor"),
        P(("rep", "dp"), "tensor"),
        P(("rep", "dp"), None),
        P(("rep", "dp")),
        P(),
        P("tensor", None),
        P("dp", "tensor", None),
        P("dp", None, "tensor"),
        P("dp", "tensor"),
        P("dp", None),
        P("dp", None),
        P("dp", "tensor"),
    )
    out_specs = (
        P(("rep", "dp"), "tensor"),
        P(("rep", "dp"), "tensor"),
        P(("rep", "dp"), None),
        P(("rep", "dp"), None),
        P(("rep", "dp"), "tensor"),
        P(("rep", "dp"), "tensor", None),
        P(("rep", "dp"), None, "tensor"),
    )
    return jax.shard_map(shards, mesh=mesh, in_specs=in_specs, out_specs=out_specs, check_vma=False)
```
